256 devices in a mesh: tm: 32 (over y, x, core), space: 8 (over z).
Axes of the slice: x: 4, y: 4, z: 8, core: 2. Of those that a mesh axis runs over, the one named last changes fastest.
Arguments:
- latent_tokens: bfloat16 [64, 1792, 2240], P('tm', 'space'), may hold values from -6 to 6
- norm_gain: float32 [2240], replicated, may hold values from 0.5 to 1.5
- w_query: bfloat16 [2240, 1120], P('tm', 'space'), may hold values from -0.125 to 0.125
- w_key: bfloat16 [2240, 1120], P('tm', 'space'), may hold values from -0.125 to 0.125
- w_value: bfloat16 [2240, 1120], P('tm', 'space'), may hold values from -0.125 to 0.125
- out_gain: float32 [1120], replicated, may hold values from 0.5 to 1.5
- block_ids: int32 [64], P('tm'), may hold values from 0 to 15, never falling along the last dimension, each value on 1 to 8 neighbouring positions
Outputs:
- attended: bfloat16 [64, 1792, 1120], P('tm', 'space')
The draws below stay inside these ranges and needn't reach their ends.
Inputs may be any that keep to these rules, and one draw needn't show every extreme that they name: `block_ids`: block numbers never fall from one frame to the next; each of the 16 blocks holds 1 to 8 frames and one holds exactly 8.
All inputs are finite; a program needn't handle non-finite values.
Results may differ from the reference program's by a relative error of at most 0.0065.
Values may be sent and summed in bfloat16 or wider, within the bound.
A program may use at most 192 MiB of HBM per device.

```python
import math
import jax
import jax.numpy as jnp
import numpy as np
from jax import lax

D = 2240
HEAD = 112
HEADS = 10
MOST = 8
HD = 1120
FRAMES = 64
FRAME_TOKENS = 1792
BLOCKS = 16


def levels(stream_key, shape, split, low, high):
    loudness, own = 1.0, jax.random.fold_in(stream_key, 6)
    for axis_at, blocks in split:
        heights = jnp.exp(jax.random.uniform(jax.random.fold_in(own, axis_at), (blocks,), jnp.float32, low / len(split), high / len(split)))
        loudness = loudness * jnp.repeat(heights, shape[axis_at] // blocks).reshape([-1 if axis == axis_at else 1 for axis in range(len(shape))])
    return loudness


def split_up(number_of, total, limit, lean):
    portions = [(1 << 20) // math.isqrt(rank ** lean) + 1 for rank in range(2, number_of + 1)]
    surplus, given = total - limit - (number_of - 1), [1] * (number_of - 1)
    while surplus > 0:
        free = [i for i in range(number_of - 1) if given[i] < limit]
        whole, remaining = sum([portions[i] for i in free]), surplus
        for i in free:
            extra = min(limit - given[i], max(1, remaining * portions[i] // whole), surplus)
            given[i] = given[i] + extra
            surplus = surplus - extra
    return np.array([limit] + given)


def ragged_sizes(own_key, number_of, total, limit, skew):
    if number_of == 2:
        one = jax.random.randint(own_key, (), max(1, total - limit), min(limit, total - 1) + 1)
        return jnp.stack([one, total - one])
    tallies = jnp.asarray(split_up(number_of, total, limit, skew), jnp.int32)
    pairs = (number_of - 1) // 2
    giver, sink = tallies[1:1 + 2 * pairs:2], tallies[2:2 + 2 * pairs:2]
    slack = jnp.minimum(giver - 1, limit - sink)
    passed = jax.random.randint(jax.random.fold_in(own_key, 1), (pairs,), 0, 1 << 20) % (slack + 1)
    tallies = tallies.at[1:1 + 2 * pairs:2].set(giver - passed).at[2:2 + 2 * pairs:2].set(sink + passed)
    return tallies[jax.random.permutation(jax.random.fold_in(own_key, 2), number_of)]


def centred(own_key, extent, scale, reach, pieces=(), kind=jnp.bfloat16):
    level = levels(own_key, extent, pieces, -0.22, 0.18) if pieces else 1.0
    entries = jax.random.normal(own_key, extent, jnp.float32) * scale * level
    return jnp.minimum(jnp.maximum(entries, -reach), reach).astype(kind)


def setup_inputs(seed: int = 0) -> dict:
    keys = jax.random.split(jax.random.key(seed), 8)
    latent_tokens = centred(keys[0], (FRAMES, FRAME_TOKENS, D), 1.0, 6.0, ((0, 32), (1, 8)))
    norm_gain = jnp.clip(1.0 + 0.1 * jax.random.normal(keys[1], (D,), jnp.float32), 0.5, 1.5)
    w_query = centred(keys[2], (D, HD), D ** -0.5, 0.125, ((0, 32), (1, 8)))
    w_key = centred(keys[3], (D, HD), D ** -0.5, 0.125, ((0, 32), (1, 8)))
    w_value = centred(keys[4], (D, HD), D ** -0.5, 0.125, ((0, 32), (1, 8)))
    out_gain = jnp.clip(1.0 + 0.1 * jax.random.normal(keys[5], (HD,), jnp.float32), 0.5, 1.5)
    block_ids = jnp.searchsorted(jnp.cumsum(ragged_sizes(keys[6], BLOCKS, FRAMES, MOST, 1)), jnp.arange(FRAMES), side="right").astype(jnp.int32)
    return {"latent_tokens": latent_tokens, "norm_gain": norm_gain, "w_query": w_query, "w_key": w_key, "w_value": w_value, "out_gain": out_gain, "block_ids": block_ids}


def normalize(frame, norm_gain):
    values = frame.astype(jnp.float32)
    meansq = lax.optimization_barrier(jnp.mean(values * values, axis=-1, keepdims=True))
    return (values * lax.rsqrt(meansq + 1e-06) * norm_gain).astype(jnp.bfloat16)

def reference(latent_tokens, norm_gain, w_query, w_key, w_value, out_gain, block_ids):

    def state_of(frame):
        normed = normalize(frame, norm_gain)
        key = jax.nn.relu(jnp.dot(normed, w_key, preferred_element_type=jnp.float32)).astype(jnp.bfloat16)
        value = jnp.dot(normed, w_value, preferred_element_type=jnp.float32).astype(jnp.bfloat16)
        key_head_rows = key.reshape(-1, HEADS, HEAD).astype(jnp.float32)
        value_head_rows = value.reshape(-1, HEADS, HEAD).astype(jnp.float32)
        return jnp.einsum('nqi,nqc->qic', key_head_rows, value_head_rows, precision=lax.Precision.HIGHEST)
    per_frame_state = lax.map(state_of, latent_tokens)
    earlier_mask = (block_ids[None, :] <= block_ids[:, None]).astype(jnp.float32)
    carried = jnp.einsum('fg,ghkv->fhkv', earlier_mask, per_frame_state, precision=lax.Precision.HIGHEST)
    head_gain = out_gain.reshape(HEADS, HEAD)

    def output_of(inputs):
        frame, running_state_sum = inputs
        normed = normalize(frame, norm_gain)
        query = jax.nn.relu(jnp.dot(normed, w_query, preferred_element_type=jnp.float32))
        query_head_rows = query.reshape(-1, HEADS, HEAD)
        numerator = jnp.einsum('apj,pjm->apm', query_head_rows, running_state_sum, precision=lax.Precision.HIGHEST)
        meansq = lax.optimization_barrier(jnp.mean(numerator * numerator, axis=-1, keepdims=True))
        result = numerator * lax.rsqrt(meansq + 1e-06) * head_gain
        return result.reshape(-1, HEADS * HEAD).astype(jnp.bfloat16)
    return lax.map(output_of, (latent_tokens, carried))
```

```python
import jax
import jax.numpy as jnp
from jax import lax
from jax.sharding import PartitionSpec as P

HEAD = 112
HEADS = 10


def gathered(weights):
    columns_full = lax.all_gather(jnp.stack(weights), "space", axis=2, tiled=True)
    return lax.all_gather(columns_full, "tm", axis=1, tiled=True)


def on_device(latent_tokens, norm_gain, w_query, w_key, w_value, out_gain, block_ids):
    frame_count, token_count, width = latent_tokens.shape
    row_count = frame_count * token_count
    values = latent_tokens.reshape(row_count, width).astype(jnp.float32)
    meansq = jnp.mean(values * values, axis=-1, keepdims=True)
    normed = (values * lax.rsqrt(meansq + 1e-06) * norm_gain).astype(jnp.bfloat16)
    pair = gathered((w_key, w_value))
    alone = gathered((w_query,))
    projected = jnp.einsum("rn,cnh->crh", normed, pair, preferred_element_type=jnp.float32)
    channels = projected.shape[2]
    headed = (frame_count, token_count, HEADS, HEAD)
    key = jax.nn.relu(projected[0]).astype(jnp.bfloat16).reshape(headed)
    value = projected[1].astype(jnp.bfloat16).reshape(headed)
    states = jnp.einsum("fthk,fthv->fhkv", key, value, preferred_element_type=jnp.float32)
    states = states.reshape(frame_count, channels, HEAD)
    mine = lax.psum_scatter(states, "space", scatter_dimension=1, tiled=True)
    everyone = lax.all_gather(mine.astype(jnp.bfloat16), "tm", tiled=True)
    all_ids = lax.all_gather(block_ids, "tm", tiled=True)
    reaches = (all_ids[None, :] <= block_ids[:, None]).astype(jnp.bfloat16)
    carried = jnp.einsum("fg,gkv->fkv", reaches, everyone, preferred_element_type=jnp.float32)
    carried = lax.all_gather(carried.astype(jnp.bfloat16), "space", axis=1, tiled=True)
    carried = carried.reshape(frame_count, HEADS, HEAD, HEAD)
    query = jnp.einsum("rn,cnh->crh", normed, alone, preferred_element_type=jnp.float32)[0]
    query = jax.nn.relu(query).astype(jnp.bfloat16).reshape(headed)
    numerator = jnp.einsum("fthk,fhkv->fthv", query, carried, preferred_element_type=jnp.float32)
    head_meansq = jnp.mean(numerator * numerator, axis=-1, keepdims=True)
    result = numerator * lax.rsqrt(head_meansq + 1e-06) * out_gain.reshape(HEADS, HEAD)
    return result.reshape(frame_count, token_count, channels).astype(jnp.bfloat16)


def solution(mesh):
    placed = (
        P("tm", "space", None),
        P(),
        P("tm", "space"),
        P("tm", "space"),
        P("tm", "space"),
        P(),
        P("tm"),
    )
    return jax.shard_map(
        on_device, mesh=mesh, in_specs=placed, out_specs=P("tm", "space", None), check_vma=False
    )
```
